32 devices in a mesh: clip: 2 (over x), trow: 8 (over z, y), tcol: 2 (over core).
Axes of the slice: x: 2, y: 2, z: 4, core: 2. Of those that a mesh axis runs over, the one named last changes fastest.
Arguments:
- field: bfloat16 [8, 2048, 8192], P(None, ('clip', 'trow'), 'tcol'), parts along dimension 1, may hold values from -6 to 6
- pointwise: bfloat16 [2, 8, 8], replicated, may hold values from -2 to 2
- mixing: bfloat16 [2, 2, 8, 8, 4608], replicated, may hold values from -2 to 2
- project: bfloat16 [8], replicated, may hold values from -2 to 2
Outputs:
- image: bfloat16 [2048, 8192], P(('clip', 'trow'), 'tcol'), parts along dimension 0
The draws below stay inside these ranges and needn't reach their ends.
There are 2 independent parts, one for each index of `clip`. The reference program is written for one: setup_inputs(seed, part) draws one part's arguments, and reference() takes and returns one part's arrays. A program takes and returns all parts, laid end to end along the dimension named above; an argument that names none is the same for every part. Nothing has to cross between parts.
All inputs are finite; a program needn't handle non-finite values.
Results may differ from the reference program's by a relative error of at most 0.0084.
Values sent between devices are 32-bit elements; how exact they have to be, the bound alone decides.
A program may use at most 128 MiB of HBM per device.

```python
import math
import jax
import jax.numpy as jnp
from jax import lax

C = 8
NY = 8192
KY = 48
LAYERS = 2
ROW_DEV = 128
MODES2 = 4608
NX = 1024
N_TROW = 8


def block_scale(key, shape, cuts, smallest, high):
    gain = 1.0
    for dim, shards_of in cuts:
        steps = jax.random.uniform(jax.random.fold_in(jax.random.fold_in(key, 6), dim), (shards_of,), jnp.float32, smallest / len(cuts), high / len(cuts))
        gain = gain * jnp.repeat(jnp.exp(steps), shape[dim] // shards_of).reshape((-1,) + (1,) * (len(shape) - 1 - dim))
    return gain


def bell_draw(key, shape, deviation, limit, shards=(), held_as=jnp.bfloat16):
    values = deviation * jax.random.normal(key, shape, jnp.float32)
    if shards:
        values = values * block_scale(key, shape, shards, -0.22, 0.18)
    return jnp.clip(values, -limit, limit).astype(held_as)


def setup_inputs(seed: int = 0, part: int = 0) -> dict:
    keys = jax.random.split(jax.random.key(seed), 5)
    part_splits = jax.random.split(jax.random.fold_in(keys[4], part), 5)
    return {
        "field": bell_draw(part_splits[0], (C, NX, NY), 1.0, 6.0, ((1, 8), (2, 2))),
        "pointwise": bell_draw(keys[1], (LAYERS, C, C), C ** -0.5, 2.0),
        "mixing": bell_draw(keys[2], (LAYERS, 2, C, C, MODES2), C ** -0.5, 2.0),
        "project": bell_draw(keys[3], (C,), C ** -0.5, 2.0),
    }


def column_table(start, count, total, modes):
    columns = start + jnp.arange(count, dtype=jnp.int32)
    freqs = jnp.arange(modes, dtype=jnp.int32)
    phase = columns[:, None] * freqs[None, :] % total
    angle = phase.astype(jnp.float32) * (2.0 * math.pi / total)
    return jnp.concatenate([jnp.cos(angle), -jnp.sin(angle)], axis=1).astype(jnp.bfloat16)

def row_tables(start, count, total, modes):
    rows_here = start + jnp.arange(count, dtype=jnp.int32)
    freqs = jnp.arange(2 * modes, dtype=jnp.int32)
    freqs = jnp.where(freqs < modes, freqs, freqs + (total - 2 * modes)).astype(jnp.int32)
    phase = freqs[:, None] * rows_here[None, :] % total
    angle = phase.astype(jnp.float32) * (2.0 * math.pi / total)
    return (jnp.cos(angle), jnp.sin(angle))

def forward_spectrum(values, row_start, total_rows, col_start, total_cols, modes):
    channels, rows_here, cols_here = values.shape
    table = column_table(col_start, cols_here, total_cols, modes)
    partial_value = jnp.dot(values.reshape(channels * rows_here, cols_here), table, preferred_element_type=jnp.float32)
    partial_value = partial_value.reshape(channels, rows_here, 2 * modes).transpose(1, 0, 2).reshape(rows_here, channels * 2 * modes)
    cosine, sine = row_tables(row_start, rows_here, total_rows, modes)
    stacked = jnp.dot(jnp.concatenate([cosine, sine], axis=0), partial_value, precision=lax.Precision.HIGHEST, preferred_element_type=jnp.float32)
    stacked = stacked.reshape(2, 2 * modes, channels, 2, modes)
    real_part = stacked[0, :, :, 0] + stacked[1, :, :, 1]
    imag_part = stacked[0, :, :, 1] - stacked[1, :, :, 0]
    spectrum = jnp.stack([real_part, imag_part]).transpose(0, 2, 1, 3).reshape(2, channels, 2 * modes * modes)
    return spectrum * (1.0 / math.sqrt(total_rows * total_cols))

def mix_modes(spectrum, weights_in):
    weights = weights_in.astype(jnp.float32)
    real_part = lax.optimization_barrier(jnp.sum(weights[0] * spectrum[0][None], axis=1)) - lax.optimization_barrier(jnp.sum(weights[1] * spectrum[1][None], axis=1))
    imag_part = lax.optimization_barrier(jnp.sum(weights[0] * spectrum[1][None], axis=1)) + lax.optimization_barrier(jnp.sum(weights[1] * spectrum[0][None], axis=1))
    return jnp.stack([real_part, imag_part])

def inverse_field(mixed, row_start, rows_here, total_rows, col_start, cols_here, total_cols, modes):
    channels = mixed.shape[1]
    arranged = mixed.reshape(2, channels, 2 * modes, modes).transpose(2, 0, 1, 3).reshape(2 * modes, 2 * channels * modes)
    cosine, sine = row_tables(row_start, rows_here, total_rows, modes)
    table = jnp.concatenate([cosine.T, sine.T], axis=0)
    stacked = jnp.dot(table, arranged, precision=lax.Precision.HIGHEST, preferred_element_type=jnp.float32)
    stacked = stacked.reshape(2, rows_here, 2, channels, modes)
    real_part = stacked[0, :, 0] - stacked[1, :, 1]
    imag_part = stacked[1, :, 0] + stacked[0, :, 1]
    hidden = jnp.stack([real_part, imag_part], axis=2).transpose(1, 0, 2, 3).reshape(channels * rows_here, 2 * modes).astype(jnp.bfloat16)
    col_tab = column_table(col_start, cols_here, total_cols, modes)
    values = jnp.dot(hidden, col_tab.T, preferred_element_type=jnp.float32) * (1.0 / modes)
    return values.reshape(channels, rows_here, cols_here)

def layer_update(values, weights, mixed, row_start, total_rows, col_start, total_cols, modes):
    channels, rows_here, cols_here = values.shape
    spectral = inverse_field(mixed, row_start, rows_here, total_rows, col_start, cols_here, total_cols, modes)
    local = jnp.dot(weights, values.reshape(channels, rows_here * cols_here), preferred_element_type=jnp.float32)
    return jnp.tanh(local.reshape(channels, rows_here, cols_here) + spectral)

def reference(field, pointwise, mixing, project):
    total_rows = ROW_DEV * N_TROW
    current = field
    result = None
    for layer in range(LAYERS):

        def add_block(carry, index):
            start = (index * ROW_DEV).astype(jnp.int32)
            piece = lax.dynamic_slice_in_dim(current, start, ROW_DEV, 1)
            return (carry + forward_spectrum(piece, start, total_rows, 0, NY, KY), None)
        empty = jnp.zeros((2, C, MODES2), jnp.float32)
        spectrum, ignored = lax.scan(add_block, empty, jnp.arange(N_TROW, dtype=jnp.int32))
        mixed = mix_modes(spectrum, mixing[layer])
        last = layer + 1 == LAYERS

        def one_block(index):
            start = (index * ROW_DEV).astype(jnp.int32)
            piece = lax.dynamic_slice_in_dim(current, start, ROW_DEV, 1)
            updated = layer_update(piece, pointwise[layer], mixed, start, total_rows, 0, NY, KY)
            if last:
                return lax.optimization_barrier(jnp.sum(project.astype(jnp.float32)[:, None, None] * updated, axis=0)).astype(jnp.bfloat16)
            return updated.astype(jnp.bfloat16)
        pieces = lax.map(one_block, jnp.arange(N_TROW, dtype=jnp.int32))
        if last:
            result = pieces.reshape(total_rows, NY)
        else:
            current = pieces.transpose(1, 0, 2, 3).reshape(C, total_rows, NY)
    return result
```

```python
import functools
import math

import jax
import jax.numpy as jnp
from jax import lax
from jax.experimental import pallas as pl
from jax.experimental.pallas import tpu as pltpu
from jax.sharding import PartitionSpec as P

KY = 48
LAYERS = 2
LANES = 128
SUB = 8
XB = 16
MESH = pl.DeviceIdType.MESH
VMEM_BYTES = 60 * 1024 * 1024


def tile_of(cols):
    for size in (512, 256, 128):
        if cols % size == 0:
            return size
    return cols


def column_rows(start, count, total):
    columns = start + jnp.arange(count, dtype=jnp.int32)
    freqs = jnp.arange(KY, dtype=jnp.int32)
    phase = freqs[:, None] * columns[None, :] % total
    angle = phase.astype(jnp.float32) * (2.0 * math.pi / total)
    cosine = jnp.cos(angle).astype(jnp.bfloat16)
    sine = (-jnp.sin(angle)).astype(jnp.bfloat16)
    blank = jnp.zeros((LANES - 2 * KY, count), jnp.bfloat16)
    return jnp.concatenate([cosine, sine, blank, sine, -cosine, blank], axis=0)


def row_tables(start, count, total, owners, per, rows):
    owner = jnp.arange(owners * rows, dtype=jnp.int32) // rows
    local = jnp.arange(owners * rows, dtype=jnp.int32) % rows
    index = owner * per + local
    valid = (local < per) & (index < 2 * KY)
    freqs = jnp.where(index < KY, index, index + (total - 2 * KY))
    freqs = jnp.where(valid, freqs, 0)
    places = start + jnp.arange(count, dtype=jnp.int32)
    phase = freqs[:, None] * places[None, :] % total
    angle = phase.astype(jnp.float32) * (2.0 * math.pi / total)
    keep = valid[:, None]
    return jnp.where(keep, jnp.cos(angle), 0.0), jnp.where(keep, jnp.sin(angle), 0.0)


def transform_rows(channels, rows_here, scale, table_ref, acc, out_ref):
    for c in range(channels):
        here = pl.ds(c * rows_here, rows_here)
        pair = jnp.concatenate([acc[here, :LANES], acc[here, LANES:]], axis=0)
        part = jnp.dot(
            table_ref[...], pair, precision=lax.Precision.HIGHEST, preferred_element_type=jnp.float32
        )
        owners = out_ref.shape[0] * out_ref.shape[1]
        part = part * scale
        out_ref[:, :, c] = part.reshape(out_ref.shape[0], out_ref.shape[1], part.shape[0] // owners, LANES)


def accumulate(value, et_ref, acc):
    acc[...] += lax.dot_general(
        value, et_ref[...], (((1,), (1,)), ((), ())), preferred_element_type=jnp.float32
    )


def forward_kernel(scale, field_ref, et_ref, table_ref, out_ref, acc):
    channels, rows_here, cols = field_ref.shape
    step = pl.program_id(0)

    @pl.when(step == 0)
    def _():
        acc[...] = jnp.zeros_like(acc)

    accumulate(field_ref[...].reshape(channels * rows_here, cols), et_ref, acc)

    @pl.when(step == pl.num_programs(0) - 1)
    def _():
        transform_rows(channels, rows_here, scale, table_ref, acc, out_ref)


def prepare_hidden(y_ref, inverse_ref, hidden):
    channels = y_ref.shape[2]
    rows_here = inverse_ref.shape[0]
    depth = inverse_ref.shape[1] // 2
    lane = lax.broadcasted_iota(jnp.int32, (depth, LANES), 1)
    for o in range(channels):
        here = y_ref[:, :, o].reshape(depth, LANES)
        turned = jnp.where(lane < KY, -pltpu.roll(here, LANES - KY, 1), pltpu.roll(here, KY, 1))
        turned = jnp.where(lane < 2 * KY, turned, 0.0)
        part = jnp.dot(
            inverse_ref[...],
            jnp.concatenate([here, turned], axis=0),
            precision=lax.Precision.HIGHEST,
            preferred_element_type=jnp.float32,
        ).astype(jnp.bfloat16)
        for block in range(rows_here // XB):
            start = (block * channels + o) * XB
            hidden[start : start + XB, :] = part[block * XB : (block + 1) * XB]


def spectral_values(et_ref, hidden, spectral):
    spectral[...] = jnp.dot(hidden[...], et_ref[:LANES, :], preferred_element_type=jnp.float32)


def block_update(block, value_ref, kron_ref, spectral):
    channels, _, cols = value_ref.shape
    size = channels * XB
    value = value_ref[:, block * XB : (block + 1) * XB, :].reshape(size, cols)
    local = jnp.dot(kron_ref[...], value, preferred_element_type=jnp.float32)
    return jnp.tanh(local + spectral[block * size : (block + 1) * size, :] * (1.0 / KY))


def middle_kernel(scale, value_ref, et_ref, y_ref, inverse_ref, kron_ref, table_ref, next_ref, out_ref, hidden, spectral, acc):
    channels, rows_here, cols = value_ref.shape
    step = pl.program_id(0)

    @pl.when(step == 0)
    def _():
        acc[...] = jnp.zeros_like(acc)
        prepare_hidden(y_ref, inverse_ref, hidden)

    spectral_values(et_ref, hidden, spectral)
    for block in range(rows_here // XB):
        updated = block_update(block, value_ref, kron_ref, spectral).astype(jnp.bfloat16)
        next_ref[:, block * XB : (block + 1) * XB, :] = updated.reshape(channels, XB, cols)
    accumulate(next_ref[...].reshape(channels * rows_here, cols), et_ref, acc)

    @pl.when(step == pl.num_programs(0) - 1)
    def _():
        transform_rows(channels, rows_here, scale, table_ref, acc, out_ref)


def last_kernel(value_ref, et_ref, y_ref, inverse_ref, kron_ref, project_ref, image_ref, hidden, spectral):
    channels, rows_here, cols = value_ref.shape

    @pl.when(pl.program_id(0) == 0)
    def _():
        prepare_hidden(y_ref, inverse_ref, hidden)

    spectral_values(et_ref, hidden, spectral)
    for block in range(rows_here // XB):
        updated = block_update(block, value_ref, kron_ref, spectral).reshape(channels, XB, cols)
        total = project_ref[0] * updated[0]
        for c in range(1, channels):
            total = total + project_ref[c] * updated[c]
        image_ref[block * XB : (block + 1) * XB, :] = total.astype(jnp.bfloat16)


def exchange_kernel(
    groups, spectrum_ref, same_ref, cross_ref, out_ref, partner_part, mine, arrived, mixed,
    pair_send, pair_recv, sum_send, sum_recv, mix_send, mix_recv, relay_send, relay_recv,
):
    clip = lax.axis_index("clip")
    row = lax.axis_index("trow")
    core = lax.axis_index("tcol")
    other = 1 - core
    channels = spectrum_ref.shape[2]

    barrier = pltpu.get_barrier_semaphore()
    pl.semaphore_signal(barrier, inc=1, device_id=(clip, row, other), device_id_type=MESH)
    for j in range(1, groups):
        peer = lax.rem(row + j, groups)
        pl.semaphore_signal(barrier, inc=1, device_id=(clip, peer, core), device_id_type=MESH)
    pl.semaphore_wait(barrier, groups)

    pair = pltpu.make_async_remote_copy(
        src_ref=spectrum_ref.at[other],
        dst_ref=partner_part,
        send_sem=pair_send,
        recv_sem=pair_recv,
        device_id=(clip, row, other),
        device_id_type=MESH,
    )
    pair.start()
    pair.wait()

    mine[...] = spectrum_ref[core] + partner_part[...]
    sums = []
    for j in range(1, groups):
        peer = lax.rem(row + j, groups)
        copy = pltpu.make_async_remote_copy(
            src_ref=mine.at[peer],
            dst_ref=arrived.at[j - 1],
            send_sem=sum_send.at[j - 1],
            recv_sem=sum_recv.at[j - 1],
            device_id=(clip, peer, core),
            device_id_type=MESH,
        )
        copy.start()
        sums.append(copy)
    total = mine[row]
    for j in range(1, groups):
        sums[j - 1].wait_recv()
        total = total + arrived[j - 1]

    lane = lax.broadcasted_iota(jnp.int32, total.shape[1:], 1)
    plain = [total[c] for c in range(channels)]
    swapped = [
        jnp.where(lane < KY, pltpu.roll(s, LANES - KY, 1), pltpu.roll(s, KY, 1)) for s in plain
    ]
    for o in range(channels):
        value = same_ref[o, 0] * plain[0] + cross_ref[o, 0] * swapped[0]
        for c in range(1, channels):
            value = value + (same_ref[o, c] * plain[c] + cross_ref[o, c] * swapped[c])
        mixed[o] = value
    out_ref[core, row] = mixed[...]

    sends = []
    for j in range(1, groups):
        peer = lax.rem(row + j, groups)
        copy = pltpu.make_async_remote_copy(
            src_ref=mixed,
            dst_ref=out_ref.at[core, row],
            send_sem=mix_send.at[j - 1],
            recv_sem=mix_recv.at[j - 1],
            device_id=(clip, peer, core),
            device_id_type=MESH,
        )
        copy.start()
        sends.append(copy)
    relays = []
    for j in range(groups):
        source = lax.rem(row + groups - j, groups)
        if j:
            sends[j - 1].wait_recv()
        relay = pltpu.make_async_remote_copy(
            src_ref=mixed if j == 0 else out_ref.at[core, source],
            dst_ref=out_ref.at[core, source],
            send_sem=relay_send.at[j],
            recv_sem=relay_recv.at[j],
            device_id=(clip, row, other),
            device_id_type=MESH,
        )
        relay.start()
        relays.append(relay)
    for copy in sums + sends:
        copy.wait_send()
    for relay in relays:
        relay.wait()


def whole(shape):
    return pl.BlockSpec(shape, lambda i: (0,) * len(shape))


def exchange(spectrum, same, cross, groups, cid):
    chunk = spectrum.shape[2:]
    dma = pltpu.SemaphoreType.DMA
    vmem = pl.BlockSpec(memory_space=pltpu.VMEM)
    links = max(groups - 1, 1)
    return pl.pallas_call(
        functools.partial(exchange_kernel, groups),
        out_shape=jax.ShapeDtypeStruct(spectrum.shape, jnp.float32),
        in_specs=[vmem, vmem, vmem],
        out_specs=vmem,
        scratch_shapes=[
            pltpu.VMEM((groups,) + chunk, jnp.float32),
            pltpu.VMEM((groups,) + chunk, jnp.float32),
            pltpu.VMEM((links,) + chunk, jnp.float32),
            pltpu.VMEM(chunk, jnp.float32),
            dma(()), dma(()), dma((links,)), dma((links,)), dma((links,)), dma((links,)),
            dma((groups,)), dma((groups,)),
        ],
        compiler_params=pltpu.CompilerParams(
            collective_id=cid, has_side_effects=True, vmem_limit_bytes=VMEM_BYTES
        ),
        name=f"exchange_{cid}",
    )(spectrum, same, cross)


def body(groups, cores, field, pointwise, mixing, project):
    channels, rows_here, cols_here = field.shape
    total_rows = rows_here * groups
    total_cols = cols_here * cores
    row_index = lax.axis_index("trow")
    core_index = lax.axis_index("tcol")
    owners = groups * cores
    per = min(p for p in range(1, 2 * KY + 1) if 2 * KY % p == 0 and p * owners >= 2 * KY)
    sub = -(-per // SUB) * SUB
    scale = 1.0 / math.sqrt(total_rows * total_cols)
    tile = tile_of(cols_here)
    steps = cols_here // tile

    columns = column_rows(core_index * cols_here, cols_here, total_cols)
    cosine, sine = row_tables(row_index * rows_here, rows_here, total_rows, owners, per, sub)
    forward_table = jnp.concatenate([cosine, sine], axis=1)
    inverse_table = jnp.concatenate([cosine.T, sine.T], axis=1)

    first = (core_index * groups + row_index) * (per * KY)
    chunk = lax.dynamic_slice_in_dim(mixing, first, per * KY, 4)
    chunk = chunk.reshape(LAYERS, 2, channels, channels, per, KY).astype(jnp.float32)
    widths = ((0, 0), (0, 0), (0, 0), (0, sub - per), (0, LANES - 2 * KY))
    same = jnp.pad(jnp.concatenate([chunk[:, 0], chunk[:, 0]], axis=-1), widths)
    cross = jnp.pad(jnp.concatenate([-chunk[:, 1], chunk[:, 1]], axis=-1), widths)
    eye = jnp.eye(XB, dtype=jnp.bfloat16)
    krons = [jnp.kron(pointwise[layer], eye) for layer in range(LAYERS)]

    spectrum_shape = (cores, groups, channels, sub, LANES)
    spectrum_type = jax.ShapeDtypeStruct(spectrum_shape, jnp.float32)
    value_spec = pl.BlockSpec((channels, rows_here, tile), lambda i: (0, 0, i))
    et_spec = pl.BlockSpec((2 * LANES, tile), lambda i: (0, i))
    hidden = pltpu.VMEM((channels * rows_here, LANES), jnp.bfloat16)
    spectral = pltpu.VMEM((channels * rows_here, tile), jnp.float32)
    acc = pltpu.VMEM((channels * rows_here, 2 * LANES), jnp.float32)
    params = pltpu.CompilerParams(dimension_semantics=("arbitrary",), vmem_limit_bytes=VMEM_BYTES)

    spectrum = pl.pallas_call(
        functools.partial(forward_kernel, scale),
        grid=(steps,),
        out_shape=spectrum_type,
        in_specs=[value_spec, et_spec, whole(forward_table.shape)],
        out_specs=whole(spectrum_shape),
        scratch_shapes=[acc],
        compiler_params=params,
        name="forward",
    )(field, columns, forward_table)

    current = field
    for layer in range(LAYERS):
        y = exchange(spectrum, same[layer], cross[layer], groups, layer)
        specs = [value_spec, et_spec, whole(spectrum_shape), whole(inverse_table.shape), whole(krons[layer].shape)]
        if layer + 1 < LAYERS:
            current, spectrum = pl.pallas_call(
                functools.partial(middle_kernel, scale),
                grid=(steps,),
                out_shape=(jax.ShapeDtypeStruct(field.shape, jnp.bfloat16), spectrum_type),
                in_specs=specs + [whole(forward_table.shape)],
                out_specs=(value_spec, whole(spectrum_shape)),
                scratch_shapes=[hidden, spectral, acc],
                compiler_params=params,
                name="middle",
            )(current, columns, y, inverse_table, krons[layer], forward_table)
        else:
            image = pl.pallas_call(
                last_kernel,
                grid=(steps,),
                out_shape=jax.ShapeDtypeStruct((rows_here, cols_here), jnp.bfloat16),
                in_specs=specs + [pl.BlockSpec(memory_space=pltpu.SMEM)],
                out_specs=pl.BlockSpec((rows_here, tile), lambda i: (0, i)),
                scratch_shapes=[hidden, spectral],
                compiler_params=params,
                name="last",
            )(current, columns, y, inverse_table, krons[layer], project.astype(jnp.float32))
    return image


def solution(mesh):
    groups, cores = mesh.shape["trow"], mesh.shape["tcol"]
    in_specs = (P(None, ("clip", "trow"), "tcol"), P(), P(), P())
    out_specs = P(("clip", "trow"), "tcol")
    return jax.shard_map(
        functools.partial(body, groups, cores), mesh=mesh, in_specs=in_specs, out_specs=out_specs, check_vma=False
    )
```

```python
import functools
import math

import jax
import jax.numpy as jnp
from jax import lax
from jax.experimental import pallas as pl
from jax.experimental.pallas import tpu as pltpu
from jax.sharding import PartitionSpec as P

KY = 48
LAYERS = 2
LANES = 128
SUB = 8
XB = 16
MESH = pl.DeviceIdType.MESH
VMEM_BYTES = 60 * 1024 * 1024


def tile_of(cols):
    for size in (512, 256, 128):
        if cols % size == 0:
            return size
    return cols


def phase_angle(columns, total):
    freqs = jnp.arange(KY, dtype=jnp.int32)
    phase = freqs[:, None] * columns[None, :] % total
    return phase.astype(jnp.float32) * (2.0 * math.pi / total)


def column_seeds(start, count, tile, total):
    coarse = phase_angle(start + jnp.arange(count // LANES, dtype=jnp.int32) * LANES, total)
    coarse = coarse.reshape(KY, count // tile, tile // LANES).transpose(1, 0, 2)
    fine = phase_angle(jnp.arange(LANES, dtype=jnp.int32), total)
    return (
        jnp.concatenate([jnp.cos(coarse), jnp.sin(coarse)], axis=1),
        jnp.concatenate([jnp.cos(fine), jnp.sin(fine)], axis=0),
    )


def row_tables(start, count, total, owners, per, rows):
    owner = jnp.arange(owners * rows, dtype=jnp.int32) // rows
    local = jnp.arange(owners * rows, dtype=jnp.int32) % rows
    index = owner * per + local
    valid = (local < per) & (index < 2 * KY)
    freqs = jnp.where(index < KY, index, index + (total - 2 * KY))
    freqs = jnp.where(valid, freqs, 0)
    places = start + jnp.arange(count, dtype=jnp.int32)
    phase = freqs[:, None] * places[None, :] % total
    angle = phase.astype(jnp.float32) * (2.0 * math.pi / total)
    keep = valid[:, None]
    return jnp.where(keep, jnp.cos(angle), 0.0), jnp.where(keep, jnp.sin(angle), 0.0)


def transform_rows(channels, rows_here, scale, table_ref, acc, out_ref):
    cores, groups = out_ref.shape[:2]
    out_ref[...] = jnp.zeros_like(out_ref)
    for c in range(channels):
        sums = acc[:, c * rows_here : (c + 1) * rows_here]
        turned = jnp.concatenate([sums[KY:], -sums[:KY]], axis=0)
        part = lax.dot_general(
            table_ref[...],
            jnp.concatenate([sums, turned], axis=1),
            (((1,), (1,)), ((), ())),
            precision=lax.Precision.HIGHEST,
            preferred_element_type=jnp.float32,
        )
        part = part * scale
        out_ref[:, :, c, :, : 2 * KY] = part.reshape(cores, groups, part.shape[0] // (cores * groups), 2 * KY)


def accumulate(value, table, acc):
    acc[...] += lax.dot_general(
        table, value, (((1,), (1,)), ((), ())), preferred_element_type=jnp.float32
    )


def forward_kernel(scale, field_ref, coarse_ref, fine_ref, table_ref, et_ref, out_ref, acc):
    channels, rows_here, cols = field_ref.shape
    step = pl.program_id(0)

    @pl.when(step == 0)
    def _():
        acc[...] = jnp.zeros_like(acc)

    cos_fine, sin_fine = fine_ref[:KY], fine_ref[KY:]
    for group in range(cols // LANES):
        cos_coarse = coarse_ref[0, :KY, group : group + 1]
        sin_coarse = coarse_ref[0, KY:, group : group + 1]
        cosine = cos_coarse * cos_fine - sin_coarse * sin_fine
        sine = sin_coarse * cos_fine + cos_coarse * sin_fine
        et_ref[:, group * LANES : (group + 1) * LANES] = jnp.concatenate([cosine, -sine], axis=0).astype(jnp.bfloat16)
    accumulate(field_ref[...].reshape(channels * rows_here, cols), et_ref[...], acc)

    @pl.when(step == pl.num_programs(0) - 1)
    def _():
        transform_rows(channels, rows_here, scale, table_ref, acc, out_ref)


def prepare_hidden(y_ref, inverse_ref, hidden):
    channels = y_ref.shape[2]
    rows_here = inverse_ref.shape[0]
    depth = inverse_ref.shape[1] // 2
    lane = lax.broadcasted_iota(jnp.int32, (depth, LANES), 1)
    for o in range(channels):
        here = y_ref[:, :, o].reshape(depth, LANES)
        turned = jnp.where(lane < KY, -pltpu.roll(here, LANES - KY, 1), pltpu.roll(here, KY, 1))
        turned = jnp.where(lane < 2 * KY, turned, 0.0)
        part = jnp.dot(
            inverse_ref[...],
            jnp.concatenate([here, turned], axis=0),
            precision=lax.Precision.HIGHEST,
            preferred_element_type=jnp.float32,
        ).astype(jnp.bfloat16)
        for block in range(rows_here // XB):
            start = (block * channels + o) * XB
            hidden[start : start + XB, :] = part[block * XB : (block + 1) * XB, : 2 * KY]


def pointwise_matrix(layer, channels, weights_ref, kron):
    row = lax.broadcasted_iota(jnp.int32, (XB, channels * XB), 0)
    lane = lax.broadcasted_iota(jnp.int32, (XB, channels * XB), 1)
    for o in range(channels):
        value = jnp.zeros((XB, channels * XB), jnp.float32)
        for c in range(channels):
            value = jnp.where(lane == row + c * XB, weights_ref[layer * channels + o, c], value)
        kron[o * XB : (o + 1) * XB, :] = value.astype(jnp.bfloat16)


def spectral_values(et_ref, hidden, spectral):
    spectral[...] = jnp.dot(hidden[...], et_ref[...], preferred_element_type=jnp.float32)


def block_update(block, value_ref, kron, spectral):
    channels, _, cols = value_ref.shape
    size = channels * XB
    value = value_ref[:, block * XB : (block + 1) * XB, :].reshape(size, cols)
    local = jnp.dot(kron[...], value, preferred_element_type=jnp.float32)
    return jnp.tanh(local + spectral[block * size : (block + 1) * size, :] * (1.0 / KY))


def middle_kernel(
    layer, scale, value_ref, et_ref, y_ref, inverse_ref, weights_ref, table_ref, next_ref, out_ref, kron, hidden, spectral, acc
):
    channels, rows_here, cols = value_ref.shape
    step = pl.program_id(0)

    @pl.when(step == 0)
    def _():
        acc[...] = jnp.zeros_like(acc)
        prepare_hidden(y_ref, inverse_ref, hidden)
        pointwise_matrix(layer, channels, weights_ref, kron)

    spectral_values(et_ref, hidden, spectral)
    for block in range(rows_here // XB):
        updated = block_update(block, value_ref, kron, spectral).astype(jnp.bfloat16)
        next_ref[:, block * XB : (block + 1) * XB, :] = updated.reshape(channels, XB, cols)
    accumulate(next_ref[...].reshape(channels * rows_here, cols), et_ref[...], acc)

    @pl.when(step == pl.num_programs(0) - 1)
    def _():
        transform_rows(channels, rows_here, scale, table_ref, acc, out_ref)


def last_kernel(layer, value_ref, et_ref, y_ref, inverse_ref, weights_ref, image_ref, kron, hidden, spectral):
    channels, rows_here, cols = value_ref.shape

    @pl.when(pl.program_id(0) == 0)
    def _():
        prepare_hidden(y_ref, inverse_ref, hidden)
        pointwise_matrix(layer, channels, weights_ref, kron)

    spectral_values(et_ref, hidden, spectral)
    for block in range(rows_here // XB):
        updated = block_update(block, value_ref, kron, spectral).reshape(channels, XB, cols)
        total = weights_ref[LAYERS * channels, 0] * updated[0]
        for c in range(1, channels):
            total = total + weights_ref[LAYERS * channels, c] * updated[c]
        image_ref[block * XB : (block + 1) * XB, :] = total.astype(jnp.bfloat16)


def exchange_kernel(
    groups, per, spectrum_ref, same_ref, cross_ref, out_ref, partner_part, mine, arrived, mixed,
    pair_send, pair_recv, sum_send, sum_recv, mix_send, mix_recv, relay_send, relay_recv,
):
    clip = lax.axis_index("clip")
    row = lax.axis_index("trow")
    core = lax.axis_index("tcol")
    other = 1 - core
    channels = spectrum_ref.shape[2]

    if per < spectrum_ref.shape[3]:
        partner_part[...] = jnp.zeros_like(partner_part)
        arrived[...] = jnp.zeros_like(arrived)
        out_ref[...] = jnp.zeros_like(out_ref)

    barrier = pltpu.get_barrier_semaphore()
    pl.semaphore_signal(barrier, inc=1, device_id=(clip, row, other), device_id_type=MESH)
    for j in range(1, groups):
        peer = lax.rem(row + j, groups)
        pl.semaphore_signal(barrier, inc=1, device_id=(clip, peer, core), device_id_type=MESH)
    pl.semaphore_wait(barrier, groups)

    def used(ref):
        return ref.at[:, pl.ds(0, per), :]

    pairs = []
    for j in range(1, groups + 1):
        peer = lax.rem(row + j, groups)
        copy = pltpu.make_async_remote_copy(
            src_ref=used(spectrum_ref.at[other, peer]),
            dst_ref=used(partner_part.at[peer]),
            send_sem=pair_send.at[j - 1],
            recv_sem=pair_recv.at[j - 1],
            device_id=(clip, row, other),
            device_id_type=MESH,
        )
        copy.start()
        pairs.append(copy)
    sums = []
    for j in range(1, groups + 1):
        peer = lax.rem(row + j, groups)
        pairs[j - 1].wait_recv()
        mine[peer] = spectrum_ref[core, peer] + partner_part[peer]
        if j < groups:
            copy = pltpu.make_async_remote_copy(
                src_ref=used(mine.at[peer]),
                dst_ref=used(arrived.at[j - 1]),
                send_sem=sum_send.at[j - 1],
                recv_sem=sum_recv.at[j - 1],
                device_id=(clip, peer, core),
                device_id_type=MESH,
            )
            copy.start()
            sums.append(copy)
    total = mine[row]
    for j in range(1, groups):
        sums[j - 1].wait_recv()
        total = total + arrived[j - 1]

    lane = lax.broadcasted_iota(jnp.int32, total.shape[1:], 1)
    plain = [total[c] for c in range(channels)]
    swapped = [
        jnp.where(lane < KY, pltpu.roll(s, LANES - KY, 1), pltpu.roll(s, KY, 1)) for s in plain
    ]
    for o in range(channels):
        value = same_ref[o, 0] * plain[0] + cross_ref[o, 0] * swapped[0]
        for c in range(1, channels):
            value = value + (same_ref[o, c] * plain[c] + cross_ref[o, c] * swapped[c])
        mixed[o] = value
    out_ref[core, row] = mixed[...]

    sends = []
    for j in range(1, groups):
        peer = lax.rem(row + j, groups)
        copy = pltpu.make_async_remote_copy(
            src_ref=used(mixed),
            dst_ref=used(out_ref.at[core, row]),
            send_sem=mix_send.at[j - 1],
            recv_sem=mix_recv.at[j - 1],
            device_id=(clip, peer, core),
            device_id_type=MESH,
        )
        copy.start()
        sends.append(copy)
    relays = []
    for j in range(groups):
        source = lax.rem(row + groups - j, groups)
        if j:
            sends[j - 1].wait_recv()
        relay = pltpu.make_async_remote_copy(
            src_ref=used(mixed if j == 0 else out_ref.at[core, source]),
            dst_ref=used(out_ref.at[core, source]),
            send_sem=relay_send.at[j],
            recv_sem=relay_recv.at[j],
            device_id=(clip, row, other),
            device_id_type=MESH,
        )
        relay.start()
        relays.append(relay)
    for copy in pairs + sums + sends:
        copy.wait_send()
    for relay in relays:
        relay.wait()


def whole(shape):
    return pl.BlockSpec(shape, lambda i: (0,) * len(shape))


def exchange(spectrum, same, cross, groups, per, cid):
    chunk = spectrum.shape[2:]
    dma = pltpu.SemaphoreType.DMA
    vmem = pl.BlockSpec(memory_space=pltpu.VMEM)
    links = max(groups - 1, 1)
    return pl.pallas_call(
        functools.partial(exchange_kernel, groups, per),
        out_shape=jax.ShapeDtypeStruct(spectrum.shape, jnp.float32),
        in_specs=[vmem, vmem, vmem],
        out_specs=vmem,
        scratch_shapes=[
            pltpu.VMEM((groups,) + chunk, jnp.float32),
            pltpu.VMEM((groups,) + chunk, jnp.float32),
            pltpu.VMEM((links,) + chunk, jnp.float32),
            pltpu.VMEM(chunk, jnp.float32),
            dma((groups,)), dma((groups,)), dma((links,)), dma((links,)), dma((links,)), dma((links,)),
            dma((groups,)), dma((groups,)),
        ],
        compiler_params=pltpu.CompilerParams(
            collective_id=cid, has_side_effects=True, vmem_limit_bytes=VMEM_BYTES
        ),
        name=f"exchange_{cid}",
    )(spectrum, same, cross)


def body(groups, cores, field, pointwise, mixing, project):
    channels, rows_here, cols_here = field.shape
    total_rows = rows_here * groups
    total_cols = cols_here * cores
    row_index = lax.axis_index("trow")
    core_index = lax.axis_index("tcol")
    owners = groups * cores
    per = min(p for p in range(1, 2 * KY + 1) if 2 * KY % p == 0 and p * owners >= 2 * KY)
    sub = -(-per // SUB) * SUB
    scale = 1.0 / math.sqrt(total_rows * total_cols)
    tile = tile_of(cols_here)
    steps = cols_here // tile

    coarse, fine = column_seeds(core_index * cols_here, cols_here, tile, total_cols)
    cosine, sine = row_tables(row_index * rows_here, rows_here, total_rows, owners, per, sub)
    forward_table = jnp.concatenate([cosine, sine], axis=1)
    inverse_table = jnp.concatenate([cosine.T, sine.T], axis=1)

    first = (core_index * groups + row_index) * (per * KY)
    chunk = lax.dynamic_slice_in_dim(mixing, first, per * KY, 4)
    chunk = chunk.reshape(LAYERS, 2, channels, channels, per, KY).astype(jnp.float32)
    widths = ((0, 0), (0, 0), (0, 0), (0, sub - per), (0, LANES - 2 * KY))
    same = jnp.pad(jnp.concatenate([chunk[:, 0], chunk[:, 0]], axis=-1), widths)
    cross = jnp.pad(jnp.concatenate([-chunk[:, 1], chunk[:, 1]], axis=-1), widths)
    weights = jnp.concatenate([pointwise.reshape(LAYERS * channels, channels), project[None]], axis=0)
    weights = weights.astype(jnp.float32)

    spectrum_shape = (cores, groups, channels, sub, LANES)
    spectrum_type = jax.ShapeDtypeStruct(spectrum_shape, jnp.float32)
    value_spec = pl.BlockSpec((channels, rows_here, tile), lambda i: (0, 0, i))
    et_spec = pl.BlockSpec((2 * KY, tile), lambda i: (0, i))
    smem = pl.BlockSpec(memory_space=pltpu.SMEM)
    kron = pltpu.VMEM((channels * XB, channels * XB), jnp.bfloat16)
    hidden = pltpu.VMEM((channels * rows_here, 2 * KY), jnp.bfloat16)
    spectral = pltpu.VMEM((channels * rows_here, tile), jnp.float32)
    acc = pltpu.VMEM((2 * KY, channels * rows_here), jnp.float32)
    params = pltpu.CompilerParams(dimension_semantics=("arbitrary",), vmem_limit_bytes=VMEM_BYTES)

    columns, spectrum = pl.pallas_call(
        functools.partial(forward_kernel, scale),
        grid=(steps,),
        out_shape=(jax.ShapeDtypeStruct((2 * KY, cols_here), jnp.bfloat16), spectrum_type),
        in_specs=[
            value_spec,
            pl.BlockSpec((1,) + coarse.shape[1:], lambda i: (i, 0, 0)),
            whole(fine.shape),
            whole(forward_table.shape),
        ],
        out_specs=(et_spec, whole(spectrum_shape)),
        scratch_shapes=[acc],
        compiler_params=params,
        name="forward",
    )(field, coarse, fine, forward_table)

    current = field
    for layer in range(LAYERS):
        y = exchange(spectrum, same[layer], cross[layer], groups, per, layer)
        specs = [value_spec, et_spec, whole(spectrum_shape), whole(inverse_table.shape), smem]
        if layer + 1 < LAYERS:
            current, spectrum = pl.pallas_call(
                functools.partial(middle_kernel, layer, scale),
                grid=(steps,),
                out_shape=(jax.ShapeDtypeStruct(field.shape, jnp.bfloat16), spectrum_type),
                in_specs=specs + [whole(forward_table.shape)],
                out_specs=(value_spec, whole(spectrum_shape)),
                scratch_shapes=[kron, hidden, spectral, acc],
                compiler_params=params,
                name="middle",
            )(current, columns, y, inverse_table, weights, forward_table)
        else:
            image = pl.pallas_call(
                functools.partial(last_kernel, layer),
                grid=(steps,),
                out_shape=jax.ShapeDtypeStruct((rows_here, cols_here), jnp.bfloat16),
                in_specs=specs,
                out_specs=pl.BlockSpec((rows_here, tile), lambda i: (0, i)),
                scratch_shapes=[kron, hidden, spectral],
                compiler_params=params,
                name="last",
            )(current, columns, y, inverse_table, weights)
    return image


def solution(mesh):
    groups, cores = mesh.shape["trow"], mesh.shape["tcol"]
    in_specs = (P(None, ("clip", "trow"), "tcol"), P(), P(), P())
    out_specs = P(("clip", "trow"), "tcol")
    return jax.shard_map(
        functools.partial(body, groups, cores), mesh=mesh, in_specs=in_specs, out_specs=out_specs, check_vma=False
    )
```

```python
import functools
import math

import jax
import jax.numpy as jnp
from jax import lax
from jax.experimental import pallas as pl
from jax.experimental.pallas import tpu as pltpu
from jax.sharding import PartitionSpec as P

KY = 48
LAYERS = 2
LANES = 128
SUB = 8
XB = 16
MESH = pl.DeviceIdType.MESH
VMEM_BYTES = 60 * 1024 * 1024


def tile_of(cols):
    for size in (512, 256, 128):
        if cols % size == 0:
            return size
    return cols


def phase_angle(columns, total):
    freqs = jnp.arange(KY, dtype=jnp.int32)
    phase = freqs[:, None] * columns[None, :] % total
    return phase.astype(jnp.float32) * (2.0 * math.pi / total)


def column_seeds(start, count, tile, total):
    coarse = phase_angle(start + jnp.arange(count // LANES, dtype=jnp.int32) * LANES, total)
    coarse = coarse.reshape(KY, count // tile, tile // LANES).transpose(1, 0, 2)
    fine = phase_angle(jnp.arange(LANES, dtype=jnp.int32), total)
    return (
        jnp.concatenate([jnp.cos(coarse), jnp.sin(coarse)], axis=1),
        jnp.concatenate([jnp.cos(fine), jnp.sin(fine)], axis=0),
    )


def row_tables(start, count, total, owners, per, rows):
    owner = jnp.arange(owners * rows, dtype=jnp.int32) // rows
    local = jnp.arange(owners * rows, dtype=jnp.int32) % rows
    index = owner * per + local
    valid = (local < per) & (index < 2 * KY)
    freqs = jnp.where(index < KY, index, index + (total - 2 * KY))
    freqs = jnp.where(valid, freqs, 0)
    places = start + jnp.arange(count, dtype=jnp.int32)
    phase = freqs[:, None] * places[None, :] % total
    angle = phase.astype(jnp.float32) * (2.0 * math.pi / total)
    keep = valid[:, None]
    return jnp.where(keep, jnp.cos(angle), 0.0), jnp.where(keep, jnp.sin(angle), 0.0)


def transform_rows(channels, rows_here, scale, table_ref, acc, out_ref):
    cores, groups = out_ref.shape[:2]
    out_ref[...] = jnp.zeros_like(out_ref)
    for c in range(channels):
        sums = acc[:, c * rows_here : (c + 1) * rows_here]
        turned = jnp.concatenate([sums[KY:], -sums[:KY]], axis=0)
        part = lax.dot_general(
            table_ref[...],
            jnp.concatenate([sums, turned], axis=1),
            (((1,), (1,)), ((), ())),
            precision=lax.Precision.HIGHEST,
            preferred_element_type=jnp.float32,
        )
        part = part * scale
        out_ref[:, :, c, :, : 2 * KY] = part.reshape(cores, groups, part.shape[0] // (cores * groups), 2 * KY)


def accumulate(value, table, acc):
    acc[...] += lax.dot_general(
        table, value, (((1,), (1,)), ((), ())), preferred_element_type=jnp.float32
    )


def forward_kernel(scale, field_ref, coarse_ref, fine_ref, table_ref, et_ref, out_ref, acc):
    channels, rows_here, cols = field_ref.shape
    step = pl.program_id(0)

    @pl.when(step == 0)
    def _():
        acc[...] = jnp.zeros_like(acc)

    cos_fine, sin_fine = fine_ref[:KY], fine_ref[KY:]
    for group in range(cols // LANES):
        cos_coarse = coarse_ref[0, :KY, group : group + 1]
        sin_coarse = coarse_ref[0, KY:, group : group + 1]
        cosine = cos_coarse * cos_fine - sin_coarse * sin_fine
        sine = sin_coarse * cos_fine + cos_coarse * sin_fine
        et_ref[:, group * LANES : (group + 1) * LANES] = jnp.concatenate([cosine, -sine], axis=0).astype(jnp.bfloat16)
    accumulate(field_ref[...].reshape(channels * rows_here, cols), et_ref[...], acc)

    @pl.when(step == pl.num_programs(0) - 1)
    def _():
        transform_rows(channels, rows_here, scale, table_ref, acc, out_ref)


def prepare_hidden(y_ref, inverse_ref, hidden):
    channels = y_ref.shape[2]
    rows_here = inverse_ref.shape[0]
    depth = inverse_ref.shape[1] // 2
    lane = lax.broadcasted_iota(jnp.int32, (depth, LANES), 1)
    for o in range(channels):
        here = y_ref[:, :, o].reshape(depth, LANES)
        turned = jnp.where(lane < KY, -pltpu.roll(here, LANES - KY, 1), pltpu.roll(here, KY, 1))
        turned = jnp.where(lane < 2 * KY, turned, 0.0)
        part = jnp.dot(
            inverse_ref[...],
            jnp.concatenate([here, turned], axis=0),
            precision=lax.Precision.HIGHEST,
            preferred_element_type=jnp.float32,
        ).astype(jnp.bfloat16)
        for block in range(rows_here // XB):
            start = (block * channels + o) * XB
            hidden[start : start + XB, :] = part[block * XB : (block + 1) * XB, : 2 * KY]


def pointwise_matrix(layer, channels, weights_ref, kron):
    row = lax.broadcasted_iota(jnp.int32, (XB, channels * XB), 0)
    lane = lax.broadcasted_iota(jnp.int32, (XB, channels * XB), 1)
    for o in range(channels):
        value = jnp.zeros((XB, channels * XB), jnp.float32)
        for c in range(channels):
            value = jnp.where(lane == row + c * XB, weights_ref[layer * channels + o, c], value)
        kron[o * XB : (o + 1) * XB, :] = value.astype(jnp.bfloat16)


def spectral_values(et_ref, hidden, spectral):
    spectral[...] = jnp.dot(hidden[...], et_ref[...], preferred_element_type=jnp.float32)


def block_update(block, value_ref, kron, spectral):
    channels, _, cols = value_ref.shape
    size = channels * XB
    value = value_ref[:, block * XB : (block + 1) * XB, :].reshape(size, cols)
    local = jnp.dot(kron[...], value, preferred_element_type=jnp.float32)
    return jnp.tanh(local + spectral[block * size : (block + 1) * size, :] * (1.0 / KY))


def middle_kernel(
    layer, scale, value_ref, et_ref, y_ref, inverse_ref, weights_ref, table_ref, next_ref, out_ref, kron, hidden, spectral, acc
):
    channels, rows_here, cols = value_ref.shape
    step = pl.program_id(0)

    @pl.when(step == 0)
    def _():
        acc[...] = jnp.zeros_like(acc)
        prepare_hidden(y_ref, inverse_ref, hidden)
        pointwise_matrix(layer, channels, weights_ref, kron)

    spectral_values(et_ref, hidden, spectral)
    for block in range(rows_here // XB):
        updated = block_update(block, value_ref, kron, spectral).astype(jnp.bfloat16)
        next_ref[:, block * XB : (block + 1) * XB, :] = updated.reshape(channels, XB, cols)
    accumulate(next_ref[...].reshape(channels * rows_here, cols), et_ref[...], acc)

    @pl.when(step == pl.num_programs(0) - 1)
    def _():
        transform_rows(channels, rows_here, scale, table_ref, acc, out_ref)


def last_kernel(layer, value_ref, et_ref, y_ref, inverse_ref, weights_ref, image_ref, kron, hidden, spectral):
    channels, rows_here, cols = value_ref.shape

    @pl.when(pl.program_id(0) == 0)
    def _():
        prepare_hidden(y_ref, inverse_ref, hidden)
        pointwise_matrix(layer, channels, weights_ref, kron)

    spectral_values(et_ref, hidden, spectral)
    for block in range(rows_here // XB):
        updated = block_update(block, value_ref, kron, spectral).reshape(channels, XB, cols)
        total = weights_ref[LAYERS * channels, 0] * updated[0]
        for c in range(1, channels):
            total = total + weights_ref[LAYERS * channels, c] * updated[c]
        image_ref[block * XB : (block + 1) * XB, :] = total.astype(jnp.bfloat16)


def exchange_kernel(
    groups, per, layer, spectrum_ref, same_ref, cross_ref, out_ref, partner_part, mine, arrived, mixed,
    pair_send, pair_recv, sum_send, sum_recv, mix_send, mix_recv, relay_send, relay_recv,
):
    clip = lax.axis_index("clip")
    row = lax.axis_index("trow")
    core = lax.axis_index("tcol")
    other = 1 - core
    channels = spectrum_ref.shape[2]

    if per < spectrum_ref.shape[3]:
        partner_part[...] = jnp.zeros_like(partner_part)
        arrived[...] = jnp.zeros_like(arrived)
        out_ref[...] = jnp.zeros_like(out_ref)

    barrier = pltpu.get_barrier_semaphore()
    pl.semaphore_signal(barrier, inc=1, device_id=(clip, row, other), device_id_type=MESH)
    for j in range(1, groups):
        peer = lax.rem(row + j, groups)
        pl.semaphore_signal(barrier, inc=1, device_id=(clip, peer, core), device_id_type=MESH)
    pl.semaphore_wait(barrier, groups)

    def used(ref):
        return ref.at[:, pl.ds(0, per), :]

    pairs = []
    for j in range(1, groups + 1):
        peer = lax.rem(row + j, groups)
        copy = pltpu.make_async_remote_copy(
            src_ref=used(spectrum_ref.at[other, peer]),
            dst_ref=used(partner_part.at[peer]),
            send_sem=pair_send.at[j - 1],
            recv_sem=pair_recv.at[j - 1],
            device_id=(clip, row, other),
            device_id_type=MESH,
        )
        copy.start()
        pairs.append(copy)
    sums = []
    for j in range(1, groups + 1):
        peer = lax.rem(row + j, groups)
        pairs[j - 1].wait_recv()
        mine[peer] = spectrum_ref[core, peer] + partner_part[peer]
        if j < groups:
            copy = pltpu.make_async_remote_copy(
                src_ref=used(mine.at[peer]),
                dst_ref=used(arrived.at[j - 1]),
                send_sem=sum_send.at[j - 1],
                recv_sem=sum_recv.at[j - 1],
                device_id=(clip, peer, core),
                device_id_type=MESH,
            )
            copy.start()
            sums.append(copy)
    total = mine[row]
    for j in range(1, groups):
        sums[j - 1].wait_recv()
        total = total + arrived[j - 1]

    lane = lax.broadcasted_iota(jnp.int32, total.shape[1:], 1)
    plain = [total[c] for c in range(channels)]
    swapped = [
        jnp.where(lane < KY, pltpu.roll(s, LANES - KY, 1), pltpu.roll(s, KY, 1)) for s in plain
    ]
    for o in range(channels):
        value = same_ref[layer, o, 0] * plain[0] + cross_ref[layer, o, 0] * swapped[0]
        for c in range(1, channels):
            value = value + (same_ref[layer, o, c] * plain[c] + cross_ref[layer, o, c] * swapped[c])
        mixed[o] = value
    out_ref[core, row] = mixed[...]

    sends = []
    for j in range(1, groups):
        peer = lax.rem(row + j, groups)
        copy = pltpu.make_async_remote_copy(
            src_ref=used(mixed),
            dst_ref=used(out_ref.at[core, row]),
            send_sem=mix_send.at[j - 1],
            recv_sem=mix_recv.at[j - 1],
            device_id=(clip, peer, core),
            device_id_type=MESH,
        )
        copy.start()
        sends.append(copy)
    relays = []
    for j in range(groups):
        source = lax.rem(row + groups - j, groups)
        if j:
            sends[j - 1].wait_recv()
        relay = pltpu.make_async_remote_copy(
            src_ref=used(mixed if j == 0 else out_ref.at[core, source]),
            dst_ref=used(out_ref.at[core, source]),
            send_sem=relay_send.at[j],
            recv_sem=relay_recv.at[j],
            device_id=(clip, row, other),
            device_id_type=MESH,
        )
        relay.start()
        relays.append(relay)
    for copy in pairs + sums + sends:
        copy.wait_send()
    for relay in relays:
        relay.wait()


def whole(shape):
    return pl.BlockSpec(shape, lambda i: (0,) * len(shape))


def exchange(spectrum, same, cross, groups, per, cid):
    chunk = spectrum.shape[2:]
    dma = pltpu.SemaphoreType.DMA
    vmem = pl.BlockSpec(memory_space=pltpu.VMEM)
    links = max(groups - 1, 1)
    return pl.pallas_call(
        functools.partial(exchange_kernel, groups, per, cid),
        out_shape=jax.ShapeDtypeStruct(spectrum.shape, jnp.float32),
        in_specs=[vmem, vmem, vmem],
        out_specs=vmem,
        scratch_shapes=[
            pltpu.VMEM((groups,) + chunk, jnp.float32),
            pltpu.VMEM((groups,) + chunk, jnp.float32),
            pltpu.VMEM((links,) + chunk, jnp.float32),
            pltpu.VMEM(chunk, jnp.float32),
            dma((groups,)), dma((groups,)), dma((links,)), dma((links,)), dma((links,)), dma((links,)),
            dma((groups,)), dma((groups,)),
        ],
        compiler_params=pltpu.CompilerParams(
            collective_id=cid, has_side_effects=True, vmem_limit_bytes=VMEM_BYTES
        ),
        name=f"exchange_{cid}",
    )(spectrum, same, cross)


def body(groups, cores, field, pointwise, mixing, project):
    channels, rows_here, cols_here = field.shape
    total_rows = rows_here * groups
    total_cols = cols_here * cores
    row_index = lax.axis_index("trow")
    core_index = lax.axis_index("tcol")
    owners = groups * cores
    per = min(p for p in range(1, 2 * KY + 1) if 2 * KY % p == 0 and p * owners >= 2 * KY)
    sub = -(-per // SUB) * SUB
    scale = 1.0 / math.sqrt(total_rows * total_cols)
    tile = tile_of(cols_here)
    steps = cols_here // tile

    coarse, fine = column_seeds(core_index * cols_here, cols_here, tile, total_cols)
    cosine, sine = row_tables(row_index * rows_here, rows_here, total_rows, owners, per, sub)
    forward_table = jnp.concatenate([cosine, sine], axis=1)
    inverse_table = jnp.concatenate([cosine.T, sine.T], axis=1)

    first = (core_index * groups + row_index) * (per * KY)
    chunk = lax.dynamic_slice_in_dim(mixing, first, per * KY, 4)
    chunk = chunk.reshape(LAYERS, 2, channels, channels, per, KY).astype(jnp.float32)
    widths = ((0, 0), (0, 0), (0, 0), (0, sub - per), (0, LANES - 2 * KY))
    same = jnp.pad(jnp.concatenate([chunk[:, 0], chunk[:, 0]], axis=-1), widths)
    cross = jnp.pad(jnp.concatenate([-chunk[:, 1], chunk[:, 1]], axis=-1), widths)
    weights = jnp.concatenate([pointwise.reshape(LAYERS * channels, channels), project[None]], axis=0)
    weights = weights.astype(jnp.float32)

    spectrum_shape = (cores, groups, channels, sub, LANES)
    spectrum_type = jax.ShapeDtypeStruct(spectrum_shape, jnp.float32)
    value_spec = pl.BlockSpec((channels, rows_here, tile), lambda i: (0, 0, i))
    et_spec = pl.BlockSpec((2 * KY, tile), lambda i: (0, i))
    smem = pl.BlockSpec(memory_space=pltpu.SMEM)
    kron = pltpu.VMEM((channels * XB, channels * XB), jnp.bfloat16)
    hidden = pltpu.VMEM((channels * rows_here, 2 * KY), jnp.bfloat16)
    spectral = pltpu.VMEM((channels * rows_here, tile), jnp.float32)
    acc = pltpu.VMEM((2 * KY, channels * rows_here), jnp.float32)
    params = pltpu.CompilerParams(dimension_semantics=("arbitrary",), vmem_limit_bytes=VMEM_BYTES)

    columns, spectrum = pl.pallas_call(
        functools.partial(forward_kernel, scale),
        grid=(steps,),
        out_shape=(jax.ShapeDtypeStruct((2 * KY, cols_here), jnp.bfloat16), spectrum_type),
        in_specs=[
            value_spec,
            pl.BlockSpec((1,) + coarse.shape[1:], lambda i: (i, 0, 0)),
            whole(fine.shape),
            whole(forward_table.shape),
        ],
        out_specs=(et_spec, whole(spectrum_shape)),
        scratch_shapes=[acc],
        compiler_params=params,
        name="forward",
    )(field, coarse, fine, forward_table)

    current = field
    for layer in range(LAYERS):
        y = exchange(spectrum, same, cross, groups, per, layer)
        specs = [value_spec, et_spec, whole(spectrum_shape), whole(inverse_table.shape), smem]
        if layer + 1 < LAYERS:
            current, spectrum = pl.pallas_call(
                functools.partial(middle_kernel, layer, scale),
                grid=(steps,),
                out_shape=(jax.ShapeDtypeStruct(field.shape, jnp.bfloat16), spectrum_type),
                in_specs=specs + [whole(forward_table.shape)],
                out_specs=(value_spec, whole(spectrum_shape)),
                scratch_shapes=[kron, hidden, spectral, acc],
                compiler_params=params,
                name="middle",
            )(current, columns, y, inverse_table, weights, forward_table)
        else:
            image = pl.pallas_call(
                functools.partial(last_kernel, layer),
                grid=(steps,),
                out_shape=jax.ShapeDtypeStruct((rows_here, cols_here), jnp.bfloat16),
                in_specs=specs,
                out_specs=pl.BlockSpec((rows_here, tile), lambda i: (0, i)),
                scratch_shapes=[kron, hidden, spectral],
                compiler_params=params,
                name="last",
            )(current, columns, y, inverse_table, weights)
    return image


def solution(mesh):
    groups, cores = mesh.shape["trow"], mesh.shape["tcol"]
    in_specs = (P(None, ("clip", "trow"), "tcol"), P(), P(), P())
    out_specs = P(("clip", "trow"), "tcol")
    return jax.shard_map(
        functools.partial(body, groups, cores), mesh=mesh, in_specs=in_specs, out_specs=out_specs, check_vma=False
    )
```
